32 devices in a mesh: ia: 4 (over y, x), ja: 2 (over core), ka: 4 (over z).
Axes of the slice: x: 2, y: 2, z: 4, core: 2. Of those that a mesh axis runs over, the one named last changes fastest.
Arguments:
- tensor: bfloat16 [128, 256, 1024], P('ia', 'ja', 'ka'), may hold values from 5 to 200
- factor_first: bfloat16 [128, 256], P('ia', ('ja', 'ka')), may hold values from 0.19921875 to 1.5
- factor_second: bfloat16 [256, 256], P('ja', ('ia', 'ka')), may hold values from 0.19921875 to 1.5
- factor_third: bfloat16 [1024, 256], P('ka', ('ia', 'ja')), may hold values from 0.19921875 to 1.5
Outputs:
- grad_first: float32 [128, 256], P('ia', ('ja', 'ka'))
- grad_second: float32 [256, 256], P('ja', ('ia', 'ka'))
- grad_third: float32 [1024, 256], P('ka', ('ia', 'ja'))
The draws below stay inside these ranges and needn't reach their ends.
All inputs are finite; a program needn't handle non-finite values.
Results may differ from the reference program's by a relative error of at most 0.005.
Values may be sent and summed in bfloat16 or wider, within the bound.
No kernel may reach another device: no remote copies, remote signals or barrier semaphores. Data moves between devices by JAX's collectives and lax.ppermute only.
A program may use at most 64 MiB of HBM per device.

```python
import math
import jax
import jax.numpy as jnp
from jax import lax

R = 256
CI = 32
NI = 128
NJ = 256
NK = 1024
N_IA = 4


def block_levels(own_key, extent, cuts, low, high):
    factor_of, own = 1.0, jax.random.fold_in(own_key, 6)
    for dim, shards_of in cuts:
        steps = jnp.exp(jax.random.uniform(jax.random.fold_in(own, dim), (shards_of,), jnp.float32, low / len(cuts), high / len(cuts)))
        factor_of = factor_of * jnp.repeat(steps, extent[dim] // shards_of).reshape([-1 if axis == dim else 1 for axis in range(len(extent))])
    return factor_of


def setup_inputs(seed: int = 0) -> dict:
    seeds = jax.random.split(jax.random.key(seed), 5)
    return {
        "tensor": jnp.clip(jnp.exp(math.log(200.0) - 3.6888795 * jax.random.uniform(seeds[0], (NI, NJ, NK), jnp.float32) ** block_levels(seeds[0], (NI, NJ, NK), ((0, 4), (1, 2), (2, 4)), -0.2, 0.2)), 5.0, 200.0).astype(jnp.bfloat16),
        "factor_first": jnp.clip(jnp.exp(math.log(1.5) - 2.018817 * jax.random.uniform(seeds[1], (NI, R), jnp.float32) ** block_levels(seeds[1], (NI, R), ((0, 4), (1, 8)), -0.2, 0.2)), 0.19921875, 1.5).astype(jnp.bfloat16),
        "factor_second": jnp.clip(jnp.exp(math.log(1.5) - 2.018817 * jax.random.uniform(seeds[2], (NJ, R), jnp.float32) ** block_levels(seeds[2], (NJ, R), ((0, 2), (1, 16)), -0.2, 0.2)), 0.19921875, 1.5).astype(jnp.bfloat16),
        "factor_third": jnp.clip(jnp.exp(math.log(1.5) - 2.018817 * jax.random.uniform(seeds[3], (NK, R), jnp.float32) ** block_levels(seeds[3], (NK, R), ((0, 4), (1, 8)), -0.2, 0.2)), 0.19921875, 1.5).astype(jnp.bfloat16),
    }


def reference(tensor, factor_first, factor_second, factor_third):
    blocks = tensor.reshape(N_IA, CI, NJ, NK)
    rows_first = factor_first.reshape(N_IA, CI, R)
    second32 = factor_second.astype(jnp.float32)
    third32 = factor_third.astype(jnp.float32)

    def one_block(carry, item):
        grad_second, grad_third = carry
        block, first_rows = item
        first32 = first_rows.astype(jnp.float32)
        khatri = (first32[:, None, :] * second32[None, :, :]).astype(jnp.bfloat16)
        khatri32 = lax.optimization_barrier(khatri).astype(jnp.float32)
        model = jnp.einsum('ijr,kr->ijk', khatri32, third32)
        deriv = ((model - block.astype(jnp.float32)) * lax.rsqrt(model)).astype(jnp.bfloat16)
        deriv32 = lax.optimization_barrier(deriv).astype(jnp.float32)
        part_third = jnp.einsum('ijk,ijr->kr', deriv32, khatri32)
        inner = jnp.einsum('ijk,kr->ijr', deriv32, third32)
        grad_first = jnp.einsum('ijr,jr->ir', inner, second32)
        part_second = jnp.einsum('ijr,ir->jr', inner, first32)
        return ((grad_second + part_second, grad_third + part_third), grad_first)
    start = (jnp.zeros((NJ, R), jnp.float32), jnp.zeros((NK, R), jnp.float32))
    (grad_second, grad_third), firsts = lax.scan(one_block, start, (blocks, rows_first))
    grad_first = firsts.reshape(NI, R) / (NJ * NK)
    return (grad_first, grad_second / (NI * NK), grad_third / (NI * NJ))
```

```python
import jax
import jax.numpy as jnp
from jax import lax
from jax.sharding import PartitionSpec as P


def _a2a(x, axes):
    n, m = x.shape
    tile = 128 * (16 if x.dtype == jnp.bfloat16 else 8)
    padded = -(-m // tile) * tile
    if padded != m:
        x = jnp.pad(x, ((0, 0), (0, padded - m)))
    y = lax.all_to_all(x.reshape(n, padded // 128, 128), axes, 0, 0, tiled=True)
    return y.reshape(n, padded)[:, :m]


def _group_size(axes):
    n = 1
    for x in axes:
        n *= lax.axis_size(x)
    return n


def gather_group(piece, axes):
    n = _group_size(axes)
    flat = piece.reshape(1, -1)
    return _a2a(jnp.broadcast_to(flat, (n, flat.shape[1])), axes)


def reduce_group(chunks, axes):
    return jnp.sum(_a2a(chunks.reshape(chunks.shape[0], -1), axes), axis=0)


def body(tensor, factor_first, factor_second, factor_third):
    nia, nja, nka = (lax.axis_size(a) for a in ("ia", "ja", "ka"))
    rows_i, rows_j, rows_k = tensor.shape
    c1, c2, c3 = factor_first.shape[1], factor_second.shape[1], factor_third.shape[1]
    rank = c1 * nja * nka
    g1 = gather_group(factor_first, ("ja", "ka"))
    full_first = g1.reshape(nja * nka, rows_i, c1).transpose(1, 0, 2).reshape(rows_i, rank)
    g2 = gather_group(factor_second, ("ia", "ka"))
    full_second = g2.reshape(nia * nka, rows_j, c2).transpose(1, 0, 2).reshape(rows_j, rank)
    g3 = gather_group(factor_third, ("ia", "ja"))
    full_third = g3.reshape(nia * nja, rows_k, c3).transpose(1, 0, 2).reshape(rows_k, rank)

    total_i = rows_i * nia
    total_j = rows_j * nja
    total_k = rows_k * nka
    first32 = full_first.astype(jnp.float32)
    second32 = full_second.astype(jnp.float32)
    khatri = (first32[:, None, :] * second32[None, :, :]).astype(jnp.bfloat16)
    khatri_flat = khatri.reshape(rows_i * rows_j, rank)
    model = jnp.einsum("mr,kr->mk", khatri_flat, full_third, preferred_element_type=jnp.float32)
    flat_data = tensor.reshape(rows_i * rows_j, rows_k).astype(jnp.float32)
    deriv = ((model - flat_data) * lax.rsqrt(model)).astype(jnp.bfloat16)
    part_third = jnp.einsum("mk,mr->kr", deriv, khatri_flat, preferred_element_type=jnp.float32)
    inner = jnp.einsum("mk,kr->mr", deriv, full_third, preferred_element_type=jnp.float32)
    inner = inner.reshape(rows_i, rows_j, rank)
    part_first = jnp.sum(inner * second32[None, :, :], axis=1) / (total_j * total_k)
    part_second = jnp.sum(inner * first32[:, None, :], axis=0) / (total_i * total_k)
    part_third = part_third / (total_i * total_j)

    s1 = part_first.reshape(rows_i, nja * nka, c1).transpose(1, 0, 2)
    s2 = part_second.reshape(rows_j, nia * nka, c2).transpose(1, 0, 2)
    s3 = part_third.reshape(rows_k, nia * nja, c3).transpose(1, 0, 2)
    grad_first = reduce_group(s1, ("ja", "ka")).reshape(rows_i, c1)
    grad_second = reduce_group(s2, ("ia", "ka")).reshape(rows_j, c2)
    grad_third = reduce_group(s3, ("ia", "ja")).reshape(rows_k, c3)
    return (grad_first, grad_second, grad_third)


def solution(mesh):
    placed = (
        P("ia", "ja", "ka"),
        P("ia", ("ja", "ka")),
        P("ja", ("ia", "ka")),
        P("ka", ("ia", "ja")),
    )
    return jax.shard_map(
        body,
        mesh=mesh,
        in_specs=placed,
        out_specs=(P("ia", ("ja", "ka")), P("ja", ("ia", "ka")), P("ka", ("ia", "ja"))),
        check_vma=False,
    )
```

```python
import jax
import jax.numpy as jnp
from jax import lax
from jax.sharding import PartitionSpec as P

GROUPS = (("ja", "ka"), ("ia", "ka"), ("ia", "ja"))


def _bits(n):
    k = n.bit_length() - 1
    assert 1 << k == n
    return k


def _bit(axis, t):
    return (lax.axis_index(axis) // (1 << t)) % 2


def _swap(x, axis, t):
    n = lax.axis_size(axis)
    return lax.ppermute(x, axis, [(i, i ^ (1 << t)) for i in range(n)])


def _exchange(items, axis, t):
    flat = [x.reshape(-1) for x in items]
    sizes = [f.shape[0] for f in flat]
    got = _swap(jnp.concatenate(flat) if len(flat) > 1 else flat[0], axis, t)
    out, off = [], 0
    for x, m in zip(items, sizes):
        out.append(got[off:off + m].reshape(x.shape))
        off += m
    return out


def gather_all(pieces):
    accs = [p[None] for p in pieces]
    for axis in ("ka", "ja", "ia"):
        for t in range(_bits(lax.axis_size(axis))):
            who = [f for f, g in enumerate(GROUPS) if axis in g]
            got = _exchange([accs[f] for f in who], axis, t)
            hi = _bit(axis, t) == 1
            for f, r in zip(who, got):
                accs[f] = jnp.where(hi, jnp.concatenate([r, accs[f]]), jnp.concatenate([accs[f], r]))
    return accs


def reduce_all(parts):
    accs = list(parts)
    for axis in ("ia", "ja", "ka"):
        for t in reversed(range(_bits(lax.axis_size(axis)))):
            who = [f for f, g in enumerate(GROUPS) if axis in g]
            hi = _bit(axis, t) == 1
            keep, send = [], []
            for f in who:
                m = accs[f].shape[0] // 2
                lo_half, hi_half = accs[f][:m], accs[f][m:]
                keep.append(jnp.where(hi, hi_half, lo_half))
                send.append(jnp.where(hi, lo_half, hi_half))
            got = _exchange(send, axis, t)
            for f, k, r in zip(who, keep, got):
                accs[f] = k + r
    return [a[0] for a in accs]


def body(tensor, factor_first, factor_second, factor_third):
    nia, nja, nka = (lax.axis_size(a) for a in ("ia", "ja", "ka"))
    rows_i, rows_j, rows_k = tensor.shape
    c1, c2, c3 = factor_first.shape[1], factor_second.shape[1], factor_third.shape[1]
    rank = c1 * nja * nka
    g1, g2, g3 = gather_all([factor_first, factor_second, factor_third])
    full_first = g1.transpose(1, 0, 2).reshape(rows_i, rank)
    full_second = g2.transpose(1, 0, 2).reshape(rows_j, rank)
    full_third = g3.transpose(1, 0, 2).reshape(rows_k, rank)

    total_i = rows_i * nia
    total_j = rows_j * nja
    total_k = rows_k * nka
    first32 = full_first.astype(jnp.float32)
    second32 = full_second.astype(jnp.float32)
    khatri = (first32[:, None, :] * second32[None, :, :]).astype(jnp.bfloat16)
    khatri_flat = khatri.reshape(rows_i * rows_j, rank)
    model = jnp.einsum("mr,kr->mk", khatri_flat, full_third, preferred_element_type=jnp.float32)
    flat_data = tensor.reshape(rows_i * rows_j, rows_k).astype(jnp.float32)
    deriv = ((model - flat_data) * lax.rsqrt(model)).astype(jnp.bfloat16)
    part_third = jnp.einsum("mk,mr->kr", deriv, khatri_flat, preferred_element_type=jnp.float32)
    inner = jnp.einsum("mk,kr->mr", deriv, full_third, preferred_element_type=jnp.float32)
    inner = inner.reshape(rows_i, rows_j, rank)
    part_first = jnp.sum(inner * second32[None, :, :], axis=1) / (total_j * total_k)
    part_second = jnp.sum(inner * first32[:, None, :], axis=0) / (total_i * total_k)
    part_third = part_third / (total_i * total_j)

    s1 = part_first.reshape(rows_i, nja * nka, c1).transpose(1, 0, 2)
    s2 = part_second.reshape(rows_j, nia * nka, c2).transpose(1, 0, 2)
    s3 = part_third.reshape(rows_k, nia * nja, c3).transpose(1, 0, 2)
    grad_first, grad_second, grad_third = reduce_all([s1, s2, s3])
    return (grad_first, grad_second, grad_third)


def solution(mesh):
    placed = (
        P("ia", "ja", "ka"),
        P("ia", ("ja", "ka")),
        P("ja", ("ia", "ka")),
        P("ka", ("ia", "ja")),
    )
    return jax.shard_map(
        body,
        mesh=mesh,
        in_specs=placed,
        out_specs=(P("ia", ("ja", "ka")), P("ja", ("ia", "ka")), P("ka", ("ia", "ja"))),
        check_vma=False,
    )
```

```python
import jax
import jax.numpy as jnp
from jax import lax
from jax.sharding import PartitionSpec as P

GROUPS = (("ja", "ka"), ("ia", "ka"), ("ia", "ja"))


def _digits(n):
    k = n.bit_length() - 1
    assert 1 << k == n
    out, t = [], 0
    while t < k:
        w = 2 if k - t >= 2 else 1
        out.append((t, 1 << w))
        t += w
    return out


def _digit(axis, t, r):
    return (lax.axis_index(axis) // (1 << t)) % r


def _exchange(items, axis, t, s):
    n = lax.axis_size(axis)
    flat = [x.reshape(-1) for x in items]
    sizes = [f.shape[0] for f in flat]
    payload = jnp.concatenate(flat) if len(flat) > 1 else flat[0]
    got = lax.ppermute(payload, axis, [(i, i ^ (s << t)) for i in range(n)])
    out, off = [], 0
    for x, m in zip(items, sizes):
        out.append(got[off:off + m].reshape(x.shape))
        off += m
    return out


def _flip_by(x, d, r):
    w = r.bit_length() - 1
    rest = x.shape[1:]
    y = x.reshape((2,) * w + rest)
    for p in range(w):
        y = jnp.where((d // (1 << p)) % 2 == 1, jnp.flip(y, w - 1 - p), y)
    return y.reshape((r,) + rest)


def _dense(x):
    flat = x.reshape(-1)
    lanes = 128 if flat.shape[0] % 128 == 0 else flat.shape[0]
    return flat.reshape(1, flat.shape[0] // lanes, lanes)


def gather_all(pieces):
    accs = [_dense(p) for p in pieces]
    for axis in ("ka", "ja", "ia"):
        for t, r in _digits(lax.axis_size(axis)):
            who = [f for f, g in enumerate(GROUPS) if axis in g]
            mine = [accs[f] for f in who]
            got = [_exchange(mine, axis, t, s) for s in range(1, r)]
            d = _digit(axis, t, r)
            for i, f in enumerate(who):
                cands = _flip_by(jnp.stack([mine[i]] + [g[i] for g in got]), d, r)
                accs[f] = cands.reshape((-1,) + cands.shape[2:])
    return accs


def reduce_all(parts):
    accs = list(parts)
    for axis in ("ia", "ja", "ka"):
        for t, r in reversed(_digits(lax.axis_size(axis))):
            who = [f for f, g in enumerate(GROUPS) if axis in g]
            d = _digit(axis, t, r)
            subs = [_flip_by(accs[f].reshape((r, accs[f].shape[0] // r) + accs[f].shape[1:]), d, r) for f in who]
            for f, sub in zip(who, subs):
                accs[f] = sub[0]
            for s in range(1, r):
                got = _exchange([sub[s] for sub in subs], axis, t, s)
                for f, g in zip(who, got):
                    accs[f] = accs[f] + g
    return [a[0] for a in accs]


def body(tensor, factor_first, factor_second, factor_third):
    nia, nja, nka = (lax.axis_size(a) for a in ("ia", "ja", "ka"))
    rows_i, rows_j, rows_k = tensor.shape
    c1, c2, c3 = factor_first.shape[1], factor_second.shape[1], factor_third.shape[1]
    rank = c1 * nja * nka
    g1, g2, g3 = gather_all([factor_first, factor_second, factor_third])
    full_first = g1.reshape(-1, rows_i, c1).transpose(1, 0, 2).reshape(rows_i, rank)
    full_second = g2.reshape(-1, rows_j, c2).transpose(1, 0, 2).reshape(rows_j, rank)
    full_third = g3.reshape(-1, rows_k, c3).transpose(1, 0, 2).reshape(rows_k, rank)

    total_i = rows_i * nia
    total_j = rows_j * nja
    total_k = rows_k * nka
    first32 = full_first.astype(jnp.float32)
    second32 = full_second.astype(jnp.float32)
    khatri = (first32[:, None, :] * second32[None, :, :]).astype(jnp.bfloat16)
    khatri_flat = khatri.reshape(rows_i * rows_j, rank)
    model = jnp.einsum("mr,kr->mk", khatri_flat, full_third, preferred_element_type=jnp.float32)
    flat_data = tensor.reshape(rows_i * rows_j, rows_k).astype(jnp.float32)
    deriv = ((model - flat_data) * lax.rsqrt(model)).astype(jnp.bfloat16)
    part_third = jnp.einsum("mk,mr->kr", deriv, khatri_flat, preferred_element_type=jnp.float32)
    inner = jnp.einsum("mk,kr->mr", deriv, full_third, preferred_element_type=jnp.float32)
    inner = inner.reshape(rows_i, rows_j, rank)
    part_first = jnp.sum(inner * second32[None, :, :], axis=1) / (total_j * total_k)
    part_second = jnp.sum(inner * first32[:, None, :], axis=0) / (total_i * total_k)
    part_third = part_third / (total_i * total_j)

    s1 = part_first.reshape(rows_i, nja * nka, c1).transpose(1, 0, 2)
    s2 = part_second.reshape(rows_j, nia * nka, c2).transpose(1, 0, 2)
    s3 = part_third.reshape(rows_k, nia * nja, c3).transpose(1, 0, 2)
    slots = [jnp.concatenate([_dense(blk) for blk in x]) for x in (s1, s2, s3)]
    g1, g2, g3 = reduce_all(slots)
    grad_first = g1.reshape(rows_i, c1)
    grad_second = g2.reshape(rows_j, c2)
    grad_third = g3.reshape(rows_k, c3)
    return (grad_first, grad_second, grad_third)


def solution(mesh):
    placed = (
        P("ia", "ja", "ka"),
        P("ia", ("ja", "ka")),
        P("ja", ("ia", "ka")),
        P("ka", ("ia", "ja")),
    )
    return jax.shard_map(
        body,
        mesh=mesh,
        in_specs=placed,
        out_specs=(P("ia", ("ja", "ka")), P("ja", ("ia", "ka")), P("ka", ("ia", "ja"))),
        check_vma=False,
    )
```

```python
import jax
import jax.numpy as jnp
from jax import lax
from jax.sharding import PartitionSpec as P

GROUPS = (("ja", "ka"), ("ia", "ka"), ("ia", "ja"))


def _digits(n):
    k = n.bit_length() - 1
    assert 1 << k == n
    out, t = [], 0
    while t < k:
        w = 2 if k - t >= 2 else 1
        out.append((t, 1 << w))
        t += w
    return out


def _digit(axis, t, r):
    return (lax.axis_index(axis) // (1 << t)) % r


def _exchange(items, axis, t, s):
    n = lax.axis_size(axis)
    flat = [x.reshape(-1) for x in items]
    sizes = [f.shape[0] for f in flat]
    payload = jnp.concatenate(flat) if len(flat) > 1 else flat[0]
    got = lax.ppermute(payload, axis, [(i, i ^ (s << t)) for i in range(n)])
    out, off = [], 0
    for x, m in zip(items, sizes):
        out.append(got[off:off + m].reshape(x.shape))
        off += m
    return out


def _flip_by(x, d, r):
    w = r.bit_length() - 1
    rest = x.shape[1:]
    y = x.reshape((2,) * w + rest)
    for p in range(w):
        y = jnp.where((d // (1 << p)) % 2 == 1, jnp.flip(y, w - 1 - p), y)
    return y.reshape((r,) + rest)


def _dense(x):
    flat = x.reshape(-1)
    lanes = 128 if flat.shape[0] % 128 == 0 else flat.shape[0]
    return flat.reshape(1, flat.shape[0] // lanes, lanes)


def gather_all(pieces):
    accs = [_dense(p) for p in pieces]
    for axis in ("ka", "ja", "ia"):
        for t, r in _digits(lax.axis_size(axis)):
            who = [f for f, g in enumerate(GROUPS) if axis in g]
            mine = [accs[f] for f in who]
            got = [_exchange(mine, axis, t, s) for s in range(1, r)]
            d = _digit(axis, t, r)
            for i, f in enumerate(who):
                cands = _flip_by(jnp.stack([mine[i]] + [g[i] for g in got]), d, r)
                accs[f] = cands.reshape((-1,) + cands.shape[2:])
    return accs


def reduce_all(parts):
    accs = list(parts)
    for axis in ("ia", "ja", "ka"):
        for t, r in reversed(_digits(lax.axis_size(axis))):
            who = [f for f, g in enumerate(GROUPS) if axis in g]
            d = _digit(axis, t, r)
            subs = [_flip_by(accs[f].reshape((r, accs[f].shape[0] // r) + accs[f].shape[1:]), d, r) for f in who]
            for f, sub in zip(who, subs):
                accs[f] = sub[0]
            for s in range(1, r):
                got = _exchange([sub[s] for sub in subs], axis, t, s)
                for f, g in zip(who, got):
                    accs[f] = accs[f] + g
    return [a[0] for a in accs]


def body(tensor, factor_first, factor_second, factor_third):
    nia, nja, nka = (lax.axis_size(a) for a in ("ia", "ja", "ka"))
    rows_i, rows_j, rows_k = tensor.shape
    c1, c2, c3 = factor_first.shape[1], factor_second.shape[1], factor_third.shape[1]
    rank = c1 * nja * nka
    g1, g2, g3 = gather_all([factor_first, factor_second, factor_third])
    full_first = g1.reshape(-1, rows_i, c1).transpose(1, 0, 2).reshape(rows_i, rank)
    full_second = g2.reshape(-1, rows_j, c2).transpose(1, 0, 2).reshape(rows_j, rank)
    full_third = g3.reshape(-1, rows_k, c3).transpose(1, 0, 2).reshape(rows_k, rank)

    total_i = rows_i * nia
    total_j = rows_j * nja
    total_k = rows_k * nka
    first32 = full_first.astype(jnp.float32)
    second32 = full_second.astype(jnp.float32)
    khatri = (first32[:, None, :] * second32[None, :, :]).astype(jnp.bfloat16)
    khatri_flat = khatri.reshape(rows_i * rows_j, rank)
    model = jnp.einsum("mr,kr->mk", khatri_flat, full_third, preferred_element_type=jnp.float32)
    flat_data = tensor.reshape(rows_i * rows_j, rows_k).astype(jnp.float32)
    deriv = ((model - flat_data) * lax.rsqrt(model)).astype(jnp.bfloat16)
    part_third = jnp.einsum("mk,mr->kr", deriv, khatri_flat, preferred_element_type=jnp.float32)
    inner = jnp.einsum("mk,kr->mr", deriv, full_third, preferred_element_type=jnp.float32)
    inner = inner.reshape(rows_i, rows_j, rank)
    part_first = jnp.sum(inner * second32[None, :, :], axis=1) / (total_j * total_k)
    part_second = jnp.sum(inner * first32[:, None, :], axis=0) / (total_i * total_k)
    part_third = part_third / (total_i * total_j)

    s1 = part_first.reshape(rows_i, nja * nka, c1).transpose(1, 0, 2)
    s2 = part_second.reshape(rows_j, nia * nka, c2).transpose(1, 0, 2)
    s3 = part_third.reshape(rows_k, nia * nja, c3).transpose(1, 0, 2)
    slots = [x.reshape((x.shape[0],) + _dense(x[0]).shape[1:]) for x in (s1, s2, s3)]
    g1, g2, g3 = reduce_all(slots)
    grad_first = g1.reshape(rows_i, c1)
    grad_second = g2.reshape(rows_j, c2)
    grad_third = g3.reshape(rows_k, c3)
    return (grad_first, grad_second, grad_third)


def solution(mesh):
    placed = (
        P("ia", "ja", "ka"),
        P("ia", ("ja", "ka")),
        P("ja", ("ia", "ka")),
        P("ka", ("ia", "ja")),
    )
    return jax.shard_map(
        body,
        mesh=mesh,
        in_specs=placed,
        out_specs=(P("ia", ("ja", "ka")), P("ja", ("ia", "ka")), P("ka", ("ia", "ja"))),
        check_vma=False,
    )
```

```python
import jax
import jax.numpy as jnp
from jax import lax
from jax.sharding import PartitionSpec as P

GROUPS = (("ja", "ka"), ("ia", "ka"), ("ia", "ja"))


def _digits(n):
    k = n.bit_length() - 1
    assert 1 << k == n
    out, t = [], 0
    while t < k:
        w = 2 if k - t >= 2 else 1
        out.append((t, 1 << w))
        t += w
    return out


def _digit(axis, t, r):
    return (lax.axis_index(axis) // (1 << t)) % r


def _exchange(items, axis, t, s):
    n = lax.axis_size(axis)
    flat = [x.reshape(-1) for x in items]
    sizes = [f.shape[0] for f in flat]
    payload = jnp.concatenate(flat) if len(flat) > 1 else flat[0]
    got = lax.ppermute(payload, axis, [(i, i ^ (s << t)) for i in range(n)])
    out, off = [], 0
    for x, m in zip(items, sizes):
        out.append(got[off:off + m].reshape(x.shape))
        off += m
    return out


def _flip_by(x, d, r):
    w = r.bit_length() - 1
    rest = x.shape[1:]
    y = x.reshape((2,) * w + rest)
    for p in range(w):
        y = jnp.where((d // (1 << p)) % 2 == 1, jnp.flip(y, w - 1 - p), y)
    return y.reshape((r,) + rest)


def _dense(x):
    flat = x.reshape(-1)
    lanes = 128 if flat.shape[0] % 128 == 0 else flat.shape[0]
    return flat.reshape(1, flat.shape[0] // lanes, lanes)


def gather_all(pieces):
    accs = [_dense(p) for p in pieces]
    for axis in ("ka", "ja", "ia"):
        for t, r in _digits(lax.axis_size(axis)):
            who = [f for f, g in enumerate(GROUPS) if axis in g]
            mine = [accs[f] for f in who]
            got = [_exchange(mine, axis, t, s) for s in range(1, r)]
            d = _digit(axis, t, r)
            for i, f in enumerate(who):
                cands = _flip_by(jnp.stack([mine[i]] + [g[i] for g in got]), d, r)
                accs[f] = cands.reshape((-1,) + cands.shape[2:])
    return accs


def reduce_all(parts):
    accs = list(parts)
    for axis in ("ia", "ja", "ka"):
        for t, r in reversed(_digits(lax.axis_size(axis))):
            who = [f for f, g in enumerate(GROUPS) if axis in g]
            d = _digit(axis, t, r)
            subs = [_flip_by(accs[f].reshape((r, accs[f].shape[0] // r) + accs[f].shape[1:]), d, r) for f in who]
            for f, sub in zip(who, subs):
                accs[f] = sub[0]
            for s in range(1, r):
                got = _exchange([sub[s] for sub in subs], axis, t, s)
                for f, g in zip(who, got):
                    accs[f] = accs[f] + g
    return [a[0] for a in accs]


def body(tensor, factor_first, factor_second, factor_third):
    nia, nja, nka = (lax.axis_size(a) for a in ("ia", "ja", "ka"))
    rows_i, rows_j, rows_k = tensor.shape
    c1, c2, c3 = factor_first.shape[1], factor_second.shape[1], factor_third.shape[1]
    rank = c1 * nja * nka
    g1, g2, g3 = gather_all([factor_first, factor_second.T, factor_third.T])
    full_first = g1.reshape(-1, rows_i, c1).transpose(1, 0, 2).reshape(rows_i, rank)
    full_second = g2.reshape(rank, rows_j).T
    full_third = g3.reshape(rank, rows_k).T

    total_i = rows_i * nia
    total_j = rows_j * nja
    total_k = rows_k * nka
    first32 = full_first.astype(jnp.float32)
    second32 = full_second.astype(jnp.float32)
    khatri = (first32[:, None, :] * second32[None, :, :]).astype(jnp.bfloat16)
    khatri_flat = khatri.reshape(rows_i * rows_j, rank)
    model = jnp.einsum("mr,kr->mk", khatri_flat, full_third, preferred_element_type=jnp.float32)
    flat_data = tensor.reshape(rows_i * rows_j, rows_k).astype(jnp.float32)
    deriv = ((model - flat_data) * lax.rsqrt(model)).astype(jnp.bfloat16)
    part_third = jnp.einsum("mk,mr->kr", deriv, khatri_flat, preferred_element_type=jnp.float32)
    inner = jnp.einsum("mk,kr->mr", deriv, full_third, preferred_element_type=jnp.float32)
    inner = inner.reshape(rows_i, rows_j, rank)
    part_first = jnp.sum(inner * second32[None, :, :], axis=1) / (total_j * total_k)
    part_second = jnp.sum(inner * first32[:, None, :], axis=0) / (total_i * total_k)
    part_third = part_third / (total_i * total_j)

    s1 = part_first.reshape(rows_i, nja * nka, c1).transpose(1, 0, 2)
    s2 = part_second.reshape(rows_j, nia * nka, c2).transpose(1, 2, 0)
    s3 = part_third.reshape(rows_k, nia * nja, c3).transpose(1, 2, 0)
    slots = [x.reshape((x.shape[0],) + _dense(x[0]).shape[1:]) for x in (s1, s2, s3)]
    g1, g2, g3 = reduce_all(slots)
    grad_first = g1.reshape(rows_i, c1)
    grad_second = g2.reshape(c2, rows_j).T
    grad_third = g3.reshape(c3, rows_k).T
    return (grad_first, grad_second, grad_third)


def solution(mesh):
    placed = (
        P("ia", "ja", "ka"),
        P("ia", ("ja", "ka")),
        P("ja", ("ia", "ka")),
        P("ka", ("ia", "ja")),
    )
    return jax.shard_map(
        body,
        mesh=mesh,
        in_specs=placed,
        out_specs=(P("ia", ("ja", "ka")), P("ja", ("ia", "ka")), P("ka", ("ia", "ja"))),
        check_vma=False,
    )
```

```python
import jax
import jax.numpy as jnp
from jax import lax
from jax.sharding import PartitionSpec as P

GROUPS = (("ja", "ka"), ("ia", "ka"), ("ia", "ja"))


def _digits(n):
    k = n.bit_length() - 1
    assert 1 << k == n
    out, t = [], 0
    while t < k:
        w = 2 if k - t >= 2 else 1
        out.append((t, 1 << w))
        t += w
    return out


def _digit(axis, t, r):
    return (lax.axis_index(axis) // (1 << t)) % r


def _exchange(items, axis, t, s):
    n = lax.axis_size(axis)
    flat = [x.reshape(-1) for x in items]
    sizes = [f.shape[0] for f in flat]
    payload = jnp.concatenate(flat) if len(flat) > 1 else flat[0]
    got = lax.ppermute(payload, axis, [(i, i ^ (s << t)) for i in range(n)])
    out, off = [], 0
    for x, m in zip(items, sizes):
        out.append(got[off:off + m].reshape(x.shape))
        off += m
    return out


def _flip_by(x, d, r):
    w = r.bit_length() - 1
    rest = x.shape[1:]
    y = x.reshape((2,) * w + rest)
    for p in range(w):
        y = jnp.where((d // (1 << p)) % 2 == 1, jnp.flip(y, w - 1 - p), y)
    return y.reshape((r,) + rest)


def _dense(x):
    flat = x.reshape(-1)
    lanes = 128 if flat.shape[0] % 128 == 0 else flat.shape[0]
    return flat.reshape(1, flat.shape[0] // lanes, lanes)


def gather_all(pieces):
    accs = [_dense(p) for p in pieces]
    for axis in ("ka", "ja", "ia"):
        for t, r in _digits(lax.axis_size(axis)):
            who = [f for f, g in enumerate(GROUPS) if axis in g]
            mine = [accs[f] for f in who]
            got = {s: _exchange(mine, axis, t, s) for s in range(r - 1, 0, -1)}
            got = [got[s] for s in range(1, r)]
            d = _digit(axis, t, r)
            for i, f in enumerate(who):
                cands = _flip_by(jnp.stack([mine[i]] + [g[i] for g in got]), d, r)
                accs[f] = cands.reshape((-1,) + cands.shape[2:])
    return accs


def reduce_all(parts):
    accs = list(parts)
    for axis in ("ia", "ja", "ka"):
        for t, r in reversed(_digits(lax.axis_size(axis))):
            who = [f for f, g in enumerate(GROUPS) if axis in g]
            d = _digit(axis, t, r)
            subs = [_flip_by(accs[f].reshape((r, accs[f].shape[0] // r) + accs[f].shape[1:]), d, r) for f in who]
            for f, sub in zip(who, subs):
                accs[f] = sub[0]
            for s in range(r - 1, 0, -1):
                got = _exchange([sub[s] for sub in subs], axis, t, s)
                for f, g in zip(who, got):
                    accs[f] = accs[f] + g
    return [a[0] for a in accs]


def body(tensor, factor_first, factor_second, factor_third):
    nia, nja, nka = (lax.axis_size(a) for a in ("ia", "ja", "ka"))
    rows_i, rows_j, rows_k = tensor.shape
    c1, c2, c3 = factor_first.shape[1], factor_second.shape[1], factor_third.shape[1]
    rank = c1 * nja * nka
    g1, g2, g3 = gather_all([factor_first, factor_second.T, factor_third.T])
    full_first = g1.reshape(-1, rows_i, c1).transpose(1, 0, 2).reshape(rows_i, rank)
    full_second = g2.reshape(rank, rows_j).T
    full_third = g3.reshape(rank, rows_k).T

    total_i = rows_i * nia
    total_j = rows_j * nja
    total_k = rows_k * nka
    first32 = full_first.astype(jnp.float32)
    second32 = full_second.astype(jnp.float32)
    khatri = (first32[:, None, :] * second32[None, :, :]).astype(jnp.bfloat16)
    khatri_flat = khatri.reshape(rows_i * rows_j, rank)
    model = jnp.einsum("mr,kr->mk", khatri_flat, full_third, preferred_element_type=jnp.float32)
    flat_data = tensor.reshape(rows_i * rows_j, rows_k).astype(jnp.float32)
    deriv = ((model - flat_data) * lax.rsqrt(model)).astype(jnp.bfloat16)
    part_third = jnp.einsum("mk,mr->kr", deriv, khatri_flat, preferred_element_type=jnp.float32)
    inner = jnp.einsum("mk,kr->mr", deriv, full_third, preferred_element_type=jnp.float32)
    inner = inner.reshape(rows_i, rows_j, rank)
    part_first = jnp.sum(inner * second32[None, :, :], axis=1) / (total_j * total_k)
    part_second = jnp.sum(inner * first32[:, None, :], axis=0) / (total_i * total_k)
    part_third = part_third / (total_i * total_j)

    s1 = part_first.reshape(rows_i, nja * nka, c1).transpose(1, 0, 2)
    s2 = part_second.reshape(rows_j, nia * nka, c2).transpose(1, 2, 0)
    s3 = part_third.reshape(rows_k, nia * nja, c3).transpose(1, 2, 0)
    slots = [x.reshape((x.shape[0],) + _dense(x[0]).shape[1:]) for x in (s1, s2, s3)]
    g1, g2, g3 = reduce_all(slots)
    grad_first = g1.reshape(rows_i, c1)
    grad_second = g2.reshape(c2, rows_j).T
    grad_third = g3.reshape(c3, rows_k).T
    return (grad_first, grad_second, grad_third)


def solution(mesh):
    placed = (
        P("ia", "ja", "ka"),
        P("ia", ("ja", "ka")),
        P("ja", ("ia", "ka")),
        P("ka", ("ia", "ja")),
    )
    return jax.shard_map(
        body,
        mesh=mesh,
        in_specs=placed,
        out_specs=(P("ia", ("ja", "ka")), P("ja", ("ia", "ka")), P("ka", ("ia", "ja"))),
        check_vma=False,
    )
```
